128 devices in a mesh: band: 8 (over y, x_lo), blk: 16 (over z, x_hi, core).
Axes of the slice: x: 4 (x_hi: 2, x_lo: 2; x = x_hi * 2 + x_lo), y: 4, z: 4, core: 2. Of those that a mesh axis runs over, the one named last changes fastest.
Arguments:
- impedance: float32 [8, 2, 6144, 6144], P('band', None, 'blk'), may hold values from -1.3 to 1.3, as said below
- adjoint_source: float32 [8, 2, 32, 6144], P('band', None, None, 'blk'), may hold values from -60 to 60
- currents: float32 [8, 2, 32, 6144], P('band', None, None, 'blk'), may hold values from -6 to 6
- sensitivity: float32 [8, 2, 6144], P('band', None, 'blk'), may hold values from -0.3 to 0.3
- owner: int32 [6144], P('blk'), may hold values from 0 to 4095
Outputs:
- adjoint_field: float32 [8, 2, 32, 6144], P('band', None, None, 'blk')
- design_gradient: float32 [4096], P(('band', 'blk'))
The draws below stay inside these ranges and needn't reach their ends.
Inputs may be any that keep to these rules, and one draw needn't show every extreme that they name: Read as a complex matrix, each band's impedance matrix is nonsingular.
All inputs are finite; a program needn't handle non-finite values.
Results may differ from the reference program's by a relative error of at most 0.00023.
Values sent between devices are 32-bit elements; how exact they have to be, the bound alone decides.
A program may use at most 192 MiB of HBM per device.

```python
import math
import jax
import jax.numpy as jnp
from jax import lax

ORDER = 6144
EXCITATIONS = 32
ITERS = 5
CYCLES = 1
DESIGN = 4096
BANDS = 8


def draw_impedance(key, part):
    keys = jax.random.split(jax.random.fold_in(key, 11), 3)
    spread = 0.3 / math.sqrt(2.0 * ORDER)
    shape = (BANDS, 2, ORDER, ORDER)
    noise = jnp.clip(jax.random.normal(keys[0], shape, jnp.float32), -6.0, 6.0) * spread
    phase = jax.random.uniform(keys[1], (BANDS, ORDER), jnp.float32, -2.3, 2.3)
    magnitude = jnp.exp(jax.random.uniform(keys[2], (BANDS, ORDER), jnp.float32, math.log(0.8), math.log(1.25)))
    diagonal = jnp.stack([magnitude * jnp.cos(phase), magnitude * jnp.sin(phase)], axis=1)
    identity = jnp.eye(ORDER, dtype=jnp.float32)
    return noise + diagonal[:, :, :, None] * identity[None, None, :, :]


def draw_adjoint_source(key, part):
    keys = jax.random.split(jax.random.fold_in(key, 23), 3)
    shape = (BANDS, 2, EXCITATIONS, ORDER)
    excitation_scale = jnp.exp(jax.random.uniform(keys[1], (BANDS, 1, EXCITATIONS, 1), jnp.float32, math.log(0.3), math.log(3.0)))
    rough_scale = jnp.exp(jax.random.uniform(keys[2], (BANDS, 1, 1, ORDER), jnp.float32, math.log(0.5), math.log(2.0)))
    position = jnp.arange(ORDER, dtype=jnp.float32) / float(ORDER - 1)
    base = jnp.clip(jax.random.normal(keys[0], shape, jnp.float32), -6.0, 6.0)
    ramp = jnp.exp(position * math.log(3.0))
    values = 0.5 * base * excitation_scale * rough_scale * ramp
    return jnp.clip(values, -60.0, 60.0)


def set_ends(entries, own_key, low, top_value):
    longest = entries.shape.index(max(entries.shape))
    spots = []
    for shift in (0, 1):
        where = [jax.random.randint(jax.random.fold_in(own_key, axis), (), 0, length) for axis, length in enumerate(entries.shape)]
        where[longest] = (where[longest] + shift) % entries.shape[longest]
        spots.append(tuple(where))
    return entries.at[spots[0]].set(low).at[spots[1]].set(top_value)


def block_scale(key, extent, pieces, least, top_value):
    def one(dim, shards_of):
        heights = jax.random.uniform(jax.random.fold_in(jax.random.fold_in(key, 6), dim), (shards_of,), jnp.float32, least / len(pieces), top_value / len(pieces))
        return jnp.repeat(jnp.exp(heights), extent[dim] // shards_of).reshape((-1,) + (1,) * (len(extent) - dim - 1))

    loudness = one(*pieces[0])
    for cut in pieces[1:]:
        loudness = loudness * one(*cut)
    return loudness


def bell_draw(stream_key, shape, scale, reach, cuts=(), kind=jnp.bfloat16):
    entries = scale * jax.random.normal(stream_key, shape, jnp.float32)
    if cuts:
        entries = entries * block_scale(stream_key, shape, cuts, -0.22, 0.18)
    return jnp.clip(entries, -reach, reach).astype(kind)


def setup_inputs(seed: int = 0) -> dict:
    streams_of = jax.random.split(jax.random.key(seed), 6)
    return {
        "impedance": draw_impedance(jax.random.fold_in(streams_of[5], 71), 0),
        "adjoint_source": draw_adjoint_source(jax.random.fold_in(streams_of[5], 71), 0),
        "currents": bell_draw(streams_of[2], (BANDS, 2, EXCITATIONS, ORDER), 1.0, 6.0, ((0, 8), (3, 16)), jnp.float32),
        "sensitivity": bell_draw(streams_of[3], (BANDS, 2, ORDER), 0.05, 0.3, ((0, 8), (2, 16)), jnp.float32),
        "owner": set_ends(jax.random.randint(streams_of[4], (ORDER,), 0, DESIGN), jax.random.fold_in(streams_of[4], 1), 0, DESIGN - 1).astype(jnp.int32),
    }


HIGH = lax.Precision.HIGHEST
EPS = 1e-12

def apply_adjoint(panel_real, panel_imag, vector):
    count = vector.shape[1]
    stacked = jnp.concatenate([vector[0], vector[1]], axis=0)
    first = jnp.dot(stacked, panel_real, precision=HIGH, preferred_element_type=jnp.float32)
    second = jnp.dot(stacked, panel_imag, precision=HIGH, preferred_element_type=jnp.float32)
    return jnp.stack([first[:count] + second[count:], first[count:] - second[:count]])

def least_squares(columns, beta):
    count = len(columns)
    cosines = []
    sines = []
    upper = []
    rhs = [beta] + [jnp.zeros_like(beta) for position in range(count)]
    for current in range(count):
        column = list(columns[current])
        for earlier in range(current):
            top = cosines[earlier] * column[earlier] + sines[earlier] * column[earlier + 1]
            column[earlier + 1] = cosines[earlier] * column[earlier + 1] - sines[earlier] * column[earlier]
            column[earlier] = top
        radius = jnp.sqrt(column[current] * column[current] + column[current + 1] * column[current + 1])
        cosines.append(column[current] / radius)
        sines.append(column[current + 1] / radius)
        column[current] = radius
        upper.append(column[:current + 1])
        rhs[current + 1] = -sines[current] * rhs[current]
        rhs[current] = cosines[current] * rhs[current]
    weights = [None] * count
    for current in reversed(range(count)):
        total = rhs[current]
        for later in range(current + 1, count):
            total = total - upper[later][current] * weights[later]
        weights[current] = total / upper[current][current]
    return weights

def orthogonalize_local(stacked, image):
    coeffs = jnp.einsum('jckn,ckn->kj', stacked, image, precision=HIGH)
    image = image - jnp.einsum('jckn,kj->ckn', stacked, coeffs, precision=HIGH)
    length = jnp.sqrt(lax.optimization_barrier(jnp.sum(image * image, axis=(0, 2))) + EPS)
    return (image, coeffs, length)

def restarted_solve(source, operator, total, orthogonalize):
    solution = jnp.zeros_like(source)
    for cycle in range(CYCLES):
        if cycle == 0:
            residual = source
        else:
            residual = source - operator(solution)
        beta = jnp.sqrt(total(lax.optimization_barrier(jnp.sum(residual * residual, axis=(0, 2)))) + EPS)
        basis = [residual / beta[None, :, None]]
        columns = []
        for current in range(ITERS):
            image = operator(basis[current])
            image, coeffs, length = orthogonalize(jnp.stack(basis), image)
            columns.append([coeffs[:, earlier] for earlier in range(current + 1)] + [length])
            if current + 1 < ITERS:
                basis.append(image / length[None, :, None])
        weights = least_squares(columns, beta)
        for current in range(ITERS):
            solution = solution + weights[current][None, :, None] * basis[current]
    return solution

def gradient_terms(adjoint, currents, sensitivity):
    sens_real = sensitivity[:, 0][:, None, :]
    sens_imag = sensitivity[:, 1][:, None, :]
    load_real = sens_real * currents[:, 0] - sens_imag * currents[:, 1]
    load_imag = sens_real * currents[:, 1] + sens_imag * currents[:, 0]
    return -lax.optimization_barrier(jnp.sum(adjoint[:, 0] * load_real + adjoint[:, 1] * load_imag, axis=(0, 1)))

def same_value(value):
    return value

def solve_band(pair):
    panel, source = pair

    def operator(vector):
        return apply_adjoint(panel[0], panel[1], vector)
    return restarted_solve(source, operator, same_value, orthogonalize_local)

def reference(impedance, adjoint_source, currents, sensitivity, owner):
    adjoint_field = lax.map(solve_band, (impedance, adjoint_source))
    terms = gradient_terms(adjoint_field, currents, sensitivity)
    design_gradient = jax.ops.segment_sum(terms, owner, num_segments=DESIGN)
    return (adjoint_field, design_gradient)
```

```python
import functools

import jax
import jax.numpy as jnp
from jax import lax
from jax.experimental import pallas as pl
from jax.experimental.pallas import tpu as pltpu
from jax.sharding import PartitionSpec as P

ITERS = 5
DESIGN = 4096
EPS = 1e-12
CHIPS = 8
BLK = 16
LANES = 128
STAGING = 3
LAG = 2
MESH = pl.DeviceIdType.MESH
F32 = jnp.float32
BF16 = jnp.bfloat16


def givens_solve(columns, beta):
    count = len(columns)
    cosines, sines, upper = [], [], []
    rhs = [beta] + [jnp.zeros_like(beta) for _ in range(count)]
    for current in range(count):
        column = list(columns[current])
        for earlier in range(current):
            top = cosines[earlier] * column[earlier] + sines[earlier] * column[earlier + 1]
            column[earlier + 1] = (
                cosines[earlier] * column[earlier + 1] - sines[earlier] * column[earlier]
            )
            column[earlier] = top
        radius = jnp.sqrt(
            column[current] * column[current] + column[current + 1] * column[current + 1]
        )
        cosines.append(column[current] / radius)
        sines.append(column[current + 1] / radius)
        column[current] = radius
        upper.append(column[: current + 1])
        rhs[current + 1] = -sines[current] * rhs[current]
        rhs[current] = cosines[current] * rhs[current]
    weights = [None] * count
    for current in reversed(range(count)):
        total = rhs[current]
        for later in range(current + 1, count):
            total = total - upper[later][current] * weights[later]
        weights[current] = total / upper[current][current]
    return weights


def kernel(
    bands,
    share,
    panel,
    source,
    currents,
    sens,
    owner,
    field,
    design,
    staging,
    high,
    low,
    lhs,
    both,
    summed,
    pair_in,
    ring_in,
    basis,
    images,
    small_out,
    small_in,
    band_out,
    band_in,
    load_sem,
    pair_send,
    pair_recv,
    ring_send,
    ring_recv,
    small_send,
    small_recv,
    band_send,
    band_recv,
):
    excite = source.shape[0] // 2
    rows = 2 * excite
    width = source.shape[1]
    chunks = width // LANES
    wide = 2 * width
    band = lax.axis_index("band")
    blk = lax.axis_index("blk")
    core = blk % 2
    partner = blk + 1 - 2 * core
    along_x = (blk // 2) % 2
    along_z = blk // 4

    def chip_of(step):
        offset = CHIPS - 1 - step
        return ((along_z + offset % 4) % 4) * 2 + (along_x + offset // 4) % 2

    def load(step):
        slot = step % STAGING
        cols = pl.ds(pl.multiple_of(chip_of(step) * wide, wide), wide)
        return pltpu.make_async_copy(panel.at[:, cols], staging.at[slot], load_sem.at[slot])

    for step in range(STAGING):
        load(step).start()

    barrier = pltpu.get_barrier_semaphore()

    def greet_blk(step, carry):
        pl.semaphore_signal(
            barrier, inc=1, device_id={"blk": (blk + step) % BLK}, device_id_type=MESH
        )
        return carry

    def greet_band(step, carry):
        pl.semaphore_signal(
            barrier, inc=1, device_id={"band": (band + step) % bands}, device_id_type=MESH
        )
        return carry

    lax.fori_loop(1, BLK, greet_blk, 0)
    if bands > 1:
        lax.fori_loop(1, bands, greet_band, 0)
    pl.semaphore_wait(barrier, BLK - 1 + bands - 1)

    def pair_copy(step, parity):
        return pltpu.make_async_remote_copy(
            src_ref=both.at[step, 1 - core],
            dst_ref=pair_in.at[parity, step],
            send_sem=pair_send.at[step],
            recv_sem=pair_recv.at[parity, step],
            device_id={"blk": partner},
            device_id_type=MESH,
        )

    def ring_copy(step, parity):
        return pltpu.make_async_remote_copy(
            src_ref=summed.at[step],
            dst_ref=ring_in.at[parity, step],
            send_sem=ring_send.at[step],
            recv_sem=ring_recv.at[parity, step],
            device_id={"blk": chip_of(step) * 2 + core},
            device_id_type=MESH,
        )

    def small_copy(step, parity):
        return pltpu.make_async_remote_copy(
            src_ref=small_out.at[parity],
            dst_ref=small_in.at[parity, step],
            send_sem=small_send.at[step],
            recv_sem=small_recv.at[parity, step],
            device_id={"blk": (blk + step) % BLK},
            device_id_type=MESH,
        )

    def band_copy(step):
        return pltpu.make_async_remote_copy(
            src_ref=band_out,
            dst_ref=band_in.at[step],
            send_sem=band_send.at[step],
            recv_sem=band_recv.at[step],
            device_id={"band": (band + step) % bands},
            device_id_type=MESH,
        )

    def small_start(parity):
        def start(step, carry):
            small_copy(step, parity).start()
            return carry

        lax.fori_loop(1, BLK, start, 0)

    def small_wait(parity):
        def wait(step, carry):
            small_copy(step, parity).wait()
            return carry

        lax.fori_loop(1, BLK, wait, 0)

    def set_lhs(pieces):
        swapped = [jnp.concatenate([p[excite:], -p[:excite]], axis=0) for p in pieces]
        for place, piece in enumerate(list(pieces) + swapped):
            cols = slice(place * LANES, (place + 1) * LANES)
            top = piece.astype(BF16)
            lhs[0:rows, cols] = top
            lhs[rows : 2 * rows, cols] = (piece - top.astype(F32)).astype(BF16)

    def split(step):
        slot = step % STAGING
        load(step).wait()

        def convert(part, carry):
            here = pl.ds(pl.multiple_of(part * 16, 16), 16)
            value = staging[slot, here, :]
            top = value.astype(BF16)
            high[step, here, :] = top
            low[step, here, :] = (value - top.astype(F32)).astype(BF16)
            return carry

        lax.fori_loop(0, 2 * width // 16, convert, 0, unroll=4)

        @pl.when(step + STAGING < CHIPS)
        def _():
            load(step + STAGING).start()

    def multiply(step):
        first = jnp.dot(lhs[...], high[step], preferred_element_type=F32)
        second = jnp.dot(lhs[0:rows, :], low[step], preferred_element_type=F32)
        image = first[:rows] + first[rows:] + second
        for dest in range(2):
            for chunk in range(chunks):
                lane = (dest * chunks + chunk) * LANES
                both[step, dest, chunk * rows : (chunk + 1) * rows, :] = image[
                    :, lane : lane + LANES
                ]

    def forward(step, parity):
        pair_copy(step, parity).wait()
        summed[step] = both[step, core] + pair_in[parity, step]

    def apply(stage):
        parity = stage % 2

        def body(step, carry):
            @pl.when(step < CHIPS)
            def _():
                if stage == 0:
                    split(step)
                multiply(step)
                pair_copy(step, parity).start()

            @pl.when(step >= LAG)
            def _():
                forward(step - LAG, parity)
                ring_copy(step - LAG, parity).start()

            return carry

        lax.fori_loop(0, CHIPS - 1 + LAG, body, 0)

    def collect(stage):
        parity = stage % 2
        forward(CHIPS - 1, parity)

        def wait(step, carry):
            ring_copy(step, parity).wait()
            return carry

        lax.fori_loop(0, CHIPS - 1, wait, 0)
        pieces = []
        for chunk in range(chunks):
            here = slice(chunk * rows, (chunk + 1) * rows)
            total = summed[CHIPS - 1, here, :]
            for step in range(CHIPS - 1):
                total = total + ring_in[parity, step, here, :]
            pieces.append(total)
        return pieces

    def get(store, index):
        return [store[index, c * rows : (c + 1) * rows, :] for c in range(chunks)]

    def put(store, index, pieces):
        for c in range(chunks):
            store[index, c * rows : (c + 1) * rows, :] = pieces[c]

    lane_of = lax.broadcasted_iota(jnp.int32, (excite, LANES), 1)
    groups = LANES // excite

    def inner_local(a, b):
        total = a[0] * b[0]
        for c in range(1, chunks):
            total = total + a[c] * b[c]
        total = total[:excite] + total[excite:]
        return jnp.sum(total, axis=1, keepdims=True)

    def small_send_products(products, parity):
        stacked = [jnp.zeros((excite, LANES), F32) for _ in range(groups)]
        for q, (a, b) in enumerate(products):
            value = inner_local(a, b)
            g, place = q % groups, q // groups
            stacked[g] = jnp.where(lane_of == place, value, stacked[g])
        tile = jnp.transpose(jnp.concatenate(stacked, axis=0))
        small_out[parity] = tile[0:8]
        small_start(parity)

    def small_result(count, parity):
        small_wait(parity)
        total = small_out[parity]
        for step in range(1, BLK):
            total = total + small_in[parity, step]
        turned = jnp.transpose(total)
        found = []
        for q in range(count):
            g, place = q % groups, q // groups
            column = turned[g * excite : (g + 1) * excite, place : place + 1]
            found.append(jnp.broadcast_to(column, (excite, LANES)))
        return found

    def tall(value):
        return jnp.concatenate([value, value], axis=0)

    def combine(lead, scale, coeffs, vectors):
        scale = tall(scale)
        out = [piece * scale for piece in lead]
        for coeff, vector in zip(coeffs, vectors):
            coeff = tall(coeff)
            out = [o - coeff * p for o, p in zip(out, vector)]
        return out

    start = [source[:, c * LANES : (c + 1) * LANES] for c in range(chunks)]
    put(basis, 0, start)
    set_lhs(start)

    norms, inverse, gram, columns = [], [], {}, []
    coeffs = []
    for stage in range(ITERS):
        parity = stage % 2
        apply(stage)
        newest = stage - 1
        if stage == 0:
            products = [(start, start)]
        else:
            if stage > 1:
                fresh = combine(
                    get(images, newest - 1),
                    inverse[newest - 1],
                    coeffs,
                    [get(basis, i) for i in range(newest)],
                )
                put(basis, newest, fresh)
            vectors = [get(basis, i) for i in range(stage)]
            products = [(v, get(images, newest)) for v in vectors]
            if stage > 1:
                products += [(v, vectors[newest]) for v in vectors]
        small_send_products(products, parity)
        found = small_result(len(products), parity)
        if stage == 0:
            gram[0, 0] = found[0]
            norms.append(jnp.sqrt(found[0] + EPS))
            inverse.append(1.0 / norms[0])
        else:
            if stage > 1:
                for i in range(stage):
                    gram[i, newest] = gram[newest, i] = found[stage + i]
                norms.append(jnp.sqrt(gram[newest, newest] + EPS))
                inverse.append(1.0 / norms[newest])
            column = [found[i] * inverse[i] * inverse[newest] for i in range(stage)]
            columns.append(column)
            coeffs = [column[i] * inverse[i] for i in range(stage)]
        pieces = collect(stage)
        if stage == 0:
            put(images, 0, pieces)
        else:
            pieces = combine(
                pieces, inverse[newest], coeffs, [get(images, i) for i in range(stage)]
            )
            put(images, stage, pieces)
        if stage + 1 < ITERS:
            set_lhs(pieces)

    last = ITERS - 1
    fresh = combine(
        get(images, last - 1), inverse[last - 1], coeffs, [get(basis, i) for i in range(last)]
    )
    put(basis, last, fresh)
    vectors = [get(basis, i) for i in range(ITERS)]
    image = get(images, last)
    products = [(v, image) for v in vectors] + [(v, fresh) for v in vectors] + [(image, image)]
    small_send_products(products, ITERS % 2)
    found = small_result(len(products), ITERS % 2)
    for i in range(ITERS):
        gram[i, last] = gram[last, i] = found[ITERS + i]
    norms.append(jnp.sqrt(gram[last, last] + EPS))
    inverse.append(1.0 / norms[last])
    column = [found[i] * inverse[i] * inverse[last] for i in range(ITERS)]
    square = found[2 * ITERS] * inverse[last] * inverse[last]
    scaled = [column[i] * inverse[i] for i in range(ITERS)]
    for i in range(ITERS):
        inside = -2.0 * column[i]
        for j in range(ITERS):
            inside = inside + gram[i, j] * inverse[i] * scaled[j]
        square = square + column[i] * inside
    columns.append(column)
    lengths = norms[1:] + [jnp.sqrt(jnp.maximum(square, 0.0) + EPS)]
    columns = [columns[j] + [lengths[j]] for j in range(ITERS)]
    weights = givens_solve(columns, norms[0])
    solved = None
    for j in range(ITERS):
        scale = tall(weights[j] * inverse[j])
        part = [scale * p for p in vectors[j]]
        solved = part if solved is None else [s + p for s, p in zip(solved, part)]

    terms = []
    for c in range(chunks):
        here = slice(c * LANES, (c + 1) * LANES)
        field[:, here] = solved[c]
        sens_r, sens_i = sens[0:1, here], sens[1:2, here]
        cur_r, cur_i = currents[0:excite, here], currents[excite:rows, here]
        load_r = sens_r * cur_r - sens_i * cur_i
        load_i = sens_r * cur_i + sens_i * cur_r
        value = solved[c][:excite] * load_r + solved[c][excite:] * load_i
        terms.append(-jnp.sum(value, axis=0, keepdims=True))
    pad = jnp.zeros((8 - chunks, LANES), F32)
    band_out[...] = jnp.concatenate(terms + [pad], axis=0)
    total = band_out[...]
    if bands > 1:

        def band_start(step, carry):
            band_copy(step).start()
            return carry

        def band_wait(step, carry):
            band_copy(step).wait()
            return carry

        lax.fori_loop(1, bands, band_start, 0)
        lax.fori_loop(1, bands, band_wait, 0)
        for step in range(1, bands):
            total = total + band_in[step]
    parity = (ITERS + 1) % 2
    small_out[parity] = jnp.concatenate(
        [total[0:chunks], owner[0:chunks, :], jnp.zeros((8 - 2 * chunks, LANES), F32)], axis=0
    )
    small_start(parity)
    small_wait(parity)
    first_design = (band * BLK + blk) * share
    mine = (first_design + lax.broadcasted_iota(jnp.int32, (share, LANES), 0)).astype(F32)
    held = jnp.zeros((share, LANES), F32)
    for step in range(BLK):
        tile = small_out[parity] if step == 0 else small_in[parity, step]
        for c in range(chunks):
            match = tile[chunks + c : chunks + c + 1] == mine
            held = held + jnp.where(match, tile[c : c + 1], 0.0)
    held = jnp.sum(held, axis=1, keepdims=True)
    row_of = lax.broadcasted_iota(jnp.int32, (share, LANES), 0)
    lane = lax.broadcasted_iota(jnp.int32, (share, LANES), 1)
    design[...] = jnp.sum(jnp.where(row_of == lane, held, 0.0), axis=0, keepdims=True)


def body(bands, impedance, adjoint_source, currents, sensitivity, owner):
    width = impedance.shape[2]
    order = impedance.shape[3]
    excite = adjoint_source.shape[2]
    rows = 2 * excite
    tall = width // LANES * rows
    wide = 2 * width
    share = DESIGN // (bands * BLK)
    vmem = pl.BlockSpec(memory_space=pltpu.VMEM)
    dma = pltpu.SemaphoreType.DMA
    chunks = width // LANES
    field, design = pl.pallas_call(
        functools.partial(kernel, bands, share),
        out_shape=(
            jax.ShapeDtypeStruct((rows, width), F32),
            jax.ShapeDtypeStruct((1, LANES), F32),
        ),
        in_specs=[pl.BlockSpec(memory_space=pl.ANY), vmem, vmem, vmem, vmem],
        out_specs=(vmem, vmem),
        scratch_shapes=[
            pltpu.VMEM((STAGING, wide, wide), F32),
            pltpu.VMEM((CHIPS, wide, wide), BF16),
            pltpu.VMEM((CHIPS, wide, wide), BF16),
            pltpu.VMEM((2 * rows, wide), BF16),
            pltpu.VMEM((CHIPS, 2, tall, LANES), F32),
            pltpu.VMEM((CHIPS, tall, LANES), F32),
            pltpu.VMEM((2, CHIPS, tall, LANES), F32),
            pltpu.VMEM((2, CHIPS - 1, tall, LANES), F32),
            pltpu.VMEM((ITERS, tall, LANES), F32),
            pltpu.VMEM((ITERS, tall, LANES), F32),
            pltpu.VMEM((2, 8, LANES), F32),
            pltpu.VMEM((2, BLK, 8, LANES), F32),
            pltpu.VMEM((8, LANES), F32),
            pltpu.VMEM((bands, 8, LANES), F32),
            dma((STAGING,)),
            dma((CHIPS,)),
            dma((2, CHIPS)),
            dma((CHIPS,)),
            dma((2, CHIPS)),
            dma((BLK,)),
            dma((2, BLK)),
            dma((bands,)),
            dma((bands,)),
        ],
        compiler_params=pltpu.CompilerParams(
            collective_id=0, has_side_effects=True, vmem_limit_bytes=60 << 20
        ),
        name="adjoint_solve",
    )(
        impedance.reshape(wide, order),
        adjoint_source.reshape(rows, width),
        currents.reshape(rows, width),
        sensitivity.reshape(2, width),
        owner.astype(F32).reshape(chunks, LANES),
    )
    return field.reshape(1, 2, excite, width), design[0, :share]


def solution(mesh):
    placed = (
        P("band", None, "blk", None),
        P("band", None, None, "blk"),
        P("band", None, None, "blk"),
        P("band", None, "blk"),
        P("blk"),
    )
    return jax.shard_map(
        functools.partial(body, mesh.shape["band"]),
        mesh=mesh,
        in_specs=placed,
        out_specs=(P("band", None, None, "blk"), P(("band", "blk"))),
        check_vma=False,
    )
```

```python
import functools

import jax
import jax.numpy as jnp
from jax import lax
from jax.experimental import pallas as pl
from jax.experimental.pallas import tpu as pltpu
from jax.sharding import PartitionSpec as P

ITERS = 5
DESIGN = 4096
EPS = 1e-12
CHIPS = 8
BLK = 16
LANES = 128
STAGING = 3
GROUPS = 2
PER_TRIP = 2
TILE = 8
BLOCK_Z = (2, 1, 3, 1, 3, 2, 0, 0)
BLOCK_X = (1, 1, 1, 0, 0, 0, 1, 0)
HOP_Z = (0, 1, 3, 1, 3, 2, 0)
HOP_X = (1, 0, 0, 0, 0, 0, 1)
RELAYED = 3
EARLY = 5
MESH = pl.DeviceIdType.MESH
F32 = jnp.float32
BF16 = jnp.bfloat16


def givens_solve(columns, beta):
    count = len(columns)
    cosines, sines, upper = [], [], []
    rhs = [beta] + [jnp.zeros_like(beta) for _ in range(count)]
    for current in range(count):
        column = list(columns[current])
        for earlier in range(current):
            top = cosines[earlier] * column[earlier] + sines[earlier] * column[earlier + 1]
            column[earlier + 1] = (
                cosines[earlier] * column[earlier + 1] - sines[earlier] * column[earlier]
            )
            column[earlier] = top
        radius = jnp.sqrt(
            column[current] * column[current] + column[current + 1] * column[current + 1]
        )
        cosines.append(column[current] / radius)
        sines.append(column[current + 1] / radius)
        column[current] = radius
        upper.append(column[: current + 1])
        rhs[current + 1] = -sines[current] * rhs[current]
        rhs[current] = cosines[current] * rhs[current]
    weights = [None] * count
    for current in reversed(range(count)):
        total = rhs[current]
        for later in range(current + 1, count):
            total = total - upper[later][current] * weights[later]
        weights[current] = total / upper[current][current]
    return weights


def pick(values, step):
    if isinstance(step, int):
        return values[step]
    total = jnp.int32(0)
    for place, value in enumerate(values):
        if value:
            total = total + jnp.where(step == place, value, 0)
    return total


def kernel(
    bands,
    share,
    panel,
    source_hbm,
    currents_hbm,
    sens_hbm,
    owner_hbm,
    field_hbm,
    design,
    source,
    currents,
    sens,
    owner,
    field,
    staging,
    high,
    low,
    lhs,
    both,
    summed,
    pair_in,
    ring_in,
    basis,
    images,
    small_out,
    small_in,
    band_out,
    band_in,
    load_sem,
    input_sem,
    field_sem,
    pair_send,
    pair_recv,
    ring_send,
    ring_recv,
    small_send,
    small_recv,
    band_send,
    band_recv,
):
    total_excite = source.shape[0] // 2
    excite = total_excite // GROUPS
    rows = 2 * excite
    width = source.shape[1]
    chunks = width // LANES
    data = chunks * rows
    payload = data + 1
    wide = 2 * width
    trips = CHIPS // PER_TRIP
    band = lax.axis_index("band")
    blk = lax.axis_index("blk")
    core = blk % 2
    partner = blk + 1 - 2 * core
    along_x = (blk // 2) % 2
    along_z = blk // 4

    def chip_of(step):
        return ((along_z + pick(BLOCK_Z, step)) % 4) * 2 + (along_x + pick(BLOCK_X, step)) % 2

    def next_chip(step):
        return ((along_z + pick(HOP_Z, step)) % 4) * 2 + (along_x + pick(HOP_X, step)) % 2

    def load(step):
        slot = step % STAGING
        cols = pl.ds(pl.multiple_of(chip_of(step) * wide, wide), wide)
        return pltpu.make_async_copy(panel.at[:, cols], staging.at[slot], load_sem.at[slot])

    pairs = [(source_hbm, source), (currents_hbm, currents), (sens_hbm, sens), (owner_hbm, owner)]
    inputs = [
        pltpu.make_async_copy(src, dst, input_sem.at[i]) for i, (src, dst) in enumerate(pairs)
    ]
    inputs[0].start()
    for step in range(STAGING):
        load(step).start()
    for copy in inputs[1:]:
        copy.start()

    barrier = pltpu.get_barrier_semaphore()

    def greet_blk(step, carry):
        pl.semaphore_signal(
            barrier, inc=1, device_id={"blk": (blk + step) % BLK}, device_id_type=MESH
        )
        return carry

    def greet_band(step, carry):
        pl.semaphore_signal(
            barrier, inc=1, device_id={"band": (band + step) % bands}, device_id_type=MESH
        )
        return carry

    lax.fori_loop(1, BLK, greet_blk, 0)
    if bands > 1:
        lax.fori_loop(1, bands, greet_band, 0)

    def arrived():
        pl.semaphore_wait(barrier, BLK - 1 + bands - 1)

    def pair_copy(group, trip, parity):
        here = pl.ds(trip * PER_TRIP, PER_TRIP)
        return pltpu.make_async_remote_copy(
            src_ref=both.at[group, 1 - core, here, pl.ds(0, payload)],
            dst_ref=pair_in.at[group, parity, here, pl.ds(0, payload)],
            send_sem=pair_send.at[group, trip],
            recv_sem=pair_recv.at[group, parity, trip],
            device_id={"blk": partner},
            device_id_type=MESH,
        )

    def ring_copy(group, step, parity, relayed):
        return pltpu.make_async_remote_copy(
            src_ref=summed.at[group, step, pl.ds(0, payload)],
            dst_ref=ring_in.at[group, parity, step, pl.ds(0, payload)],
            send_sem=ring_send.at[group],
            recv_sem=ring_recv.at[group, parity, relayed],
            device_id={"blk": next_chip(step) * 2 + core},
            device_id_type=MESH,
        )

    def ring_whole(group, parity, first, count, relayed):
        whole = ring_in.at[group, parity, pl.ds(first, count), pl.ds(0, payload)]
        return pltpu.make_async_remote_copy(
            src_ref=whole,
            dst_ref=whole,
            send_sem=ring_send.at[group],
            recv_sem=ring_recv.at[group, parity, relayed],
            device_id={"blk": partner},
            device_id_type=MESH,
        )

    def small_copy(n, use):
        dz, dx, dc = (2, 1, 3, 0)[n // 4], 1 - (n // 2) % 2, 1 - n % 2
        target = ((along_z + dz) % 4) * 4 + ((along_x + dx) % 2) * 2 + (core + dc) % 2
        return pltpu.make_async_remote_copy(
            src_ref=small_out.at[use],
            dst_ref=small_in.at[use, n],
            send_sem=small_send.at[use],
            recv_sem=small_recv.at[use],
            device_id={"blk": target},
            device_id_type=MESH,
        )

    def band_copy(step):
        return pltpu.make_async_remote_copy(
            src_ref=band_out,
            dst_ref=band_in.at[step],
            send_sem=band_send.at[step],
            recv_sem=band_recv.at[step],
            device_id={"band": (band + step) % bands},
            device_id_type=MESH,
        )

    def small_start(use):
        for n in range(BLK - 1):
            small_copy(n, use).start()

    def small_wait(use):
        pltpu.make_async_remote_copy(
            src_ref=small_in.at[use],
            dst_ref=small_in.at[use],
            send_sem=small_send.at[use],
            recv_sem=small_recv.at[use],
            device_id={"blk": partner},
            device_id_type=MESH,
        ).wait()
        total = small_out[use]
        for n in range(BLK - 1):
            total = total + small_in[use, n]
        return total

    def set_lhs(group, pieces):
        swapped = [jnp.concatenate([p[excite:], -p[:excite]], axis=0) for p in pieces]
        for place, piece in enumerate(list(pieces) + swapped):
            cols = slice(place * LANES, (place + 1) * LANES)
            top = piece.astype(BF16)
            lhs[0, group * rows : (group + 1) * rows, cols] = top
            lhs[1, group * rows : (group + 1) * rows, cols] = (piece - top.astype(F32)).astype(
                BF16
            )

    def split(step):
        slot = step % STAGING
        load(step).wait()

        def convert(part, carry):
            here = pl.ds(pl.multiple_of(part * 16, 16), 16)
            value = staging[slot, here, :]
            top = value.astype(BF16)
            high[step, here, :] = top
            low[step, here, :] = (value - top.astype(F32)).astype(BF16)
            return carry

        lax.fori_loop(0, 2 * width // 16, convert, 0, unroll=4)

        @pl.when(step + STAGING < CHIPS)
        def _():
            load(step + STAGING).start()

    def multiply(groups, step):
        span = slice(groups[0] * rows, (groups[-1] + 1) * rows)
        count = len(groups) * rows
        left = jnp.concatenate([lhs[0, span, :], lhs[1, span, :]], axis=0)
        first = jnp.dot(left, high[step], preferred_element_type=F32)
        second = jnp.dot(lhs[0, span, :], low[step], preferred_element_type=F32)
        image = first[:count] + first[count:] + second
        for place, group in enumerate(groups):
            for dest in range(2):
                for chunk in range(chunks):
                    lane = (dest * chunks + chunk) * LANES
                    both[group, dest, step, chunk * rows : (chunk + 1) * rows, :] = image[
                        place * rows : (place + 1) * rows, lane : lane + LANES
                    ]

    def add_pair(group, trip, parity):
        pair_copy(group, trip, parity).wait()
        for part in range(PER_TRIP):
            step = trip * PER_TRIP + part
            summed[group, step] = both[group, core, step] + pair_in[group, parity, step]

    def forward(group, trip, parity):
        add_pair(group, trip, parity)
        for part in range(PER_TRIP):
            step = trip * PER_TRIP + part

            @pl.when(step < RELAYED)
            def _():
                ring_copy(group, step, parity, 1).start()

            @pl.when((step >= RELAYED) & (step < EARLY))
            def _():
                ring_copy(group, step, parity, 0).start()

    def finish(group, parity):
        ring_whole(group, parity, 0, RELAYED, 1).wait_recv()
        across, along = EARLY, EARLY + 1
        summed[group, across] = summed[group, across] + ring_in[group, parity, 0]
        ring_copy(group, across, parity, 0).start()
        summed[group, along] = (
            summed[group, along] + ring_in[group, parity, 1] + ring_in[group, parity, 2]
        )
        ring_copy(group, along, parity, 0).start()

    def flush(group, stage):
        add_pair(group, trips - 1, stage % 2)
        finish(group, stage % 2)

    def apply(groups, stage, pending):
        parity = stage % 2

        def body(trip, carry):
            for part in range(PER_TRIP):
                if stage == 0:
                    split(trip * PER_TRIP + part)
            for part in range(PER_TRIP):
                multiply(groups, trip * PER_TRIP + part)
            for group in groups:
                pair_copy(group, trip, parity).start()

            @pl.when(trip > 0)
            def _():
                for group in groups:
                    forward(group, trip - 1, parity)

            if pending is not None:

                @pl.when(trip == 0)
                def _():
                    flush(*pending)

            return carry

        lax.fori_loop(0, trips, body, 0)

    def collect(group, stage):
        parity = stage % 2
        ring_whole(group, parity, RELAYED, CHIPS - 1 - RELAYED, 0).wait_recv()
        ring_whole(group, parity, 0, CHIPS - 1, 0).wait_send()

        def gather(here):
            total = summed[group, CHIPS - 1, here, :]
            for step in range(RELAYED, CHIPS - 1):
                total = total + ring_in[group, parity, step, here, :]
            return total

        tile = gather(slice(data, data + 1))
        pieces = [gather(slice(c * rows, (c + 1) * rows)) for c in range(chunks)]
        return pieces, tile

    def get(store, group, index):
        return [store[group, index, c * rows : (c + 1) * rows, :] for c in range(chunks)]

    def put(store, group, index, pieces):
        for c in range(chunks):
            store[group, index, c * rows : (c + 1) * rows, :] = pieces[c]

    lane_of = lax.broadcasted_iota(jnp.int32, (excite, LANES), 1)
    row_of = lax.broadcasted_iota(jnp.int32, (excite, LANES), 0)
    segments = LANES // excite

    def inner_local(a, b):
        total = a[0] * b[0]
        for c in range(1, chunks):
            total = total + a[c] * b[c]
        total = total[:excite] + total[excite:]
        return jnp.sum(total, axis=1, keepdims=True)

    def pack(products):
        lines = []
        for first in range(0, len(products), segments):
            line = jnp.zeros((excite, LANES), F32)
            for q, (a, b) in enumerate(products[first : first + segments]):
                line = jnp.where(lane_of == row_of + q * excite, inner_local(a, b), line)
            lines.append(jnp.sum(line, axis=0, keepdims=True))
        lines.append(jnp.zeros((TILE - len(lines), LANES), F32))
        return jnp.concatenate(lines, axis=0)

    def unpack(tile, count):
        found = []
        for q in range(count):
            line = tile[q // segments : q // segments + 1]
            picked = jnp.where(lane_of == row_of + (q % segments) * excite, line, 0.0)
            value = jnp.sum(picked, axis=1, keepdims=True)
            found.append(jnp.broadcast_to(value, (excite, LANES)))
        return found

    def stamp(group, tile):
        for step in range(CHIPS):
            for dest in range(2):
                both[group, dest, step, data : data + TILE, :] = tile

    def tall(value):
        return jnp.concatenate([value, value], axis=0)

    def combine(lead, scale, coeffs, vectors):
        scale = tall(scale)
        out = [piece * scale for piece in lead]
        for coeff, vector in zip(coeffs, vectors):
            coeff = tall(coeff)
            out = [o - coeff * p for o, p in zip(out, vector)]
        return out

    def source_rows(ref, group, here):
        first = group * excite
        return jnp.concatenate(
            [
                ref[first : first + excite, here],
                ref[total_excite + first : total_excite + first + excite, here],
            ],
            axis=0,
        )

    def begin(group):
        start = [
            source_rows(source, group, slice(c * LANES, (c + 1) * LANES)) for c in range(chunks)
        ]
        put(basis, group, 0, start)
        set_lhs(group, start)
        stamp(group, pack([(start, start)]))
        return {"norms": [], "inverse": [], "gram": {}, "columns": []}

    def absorb(group, stage, state):
        pieces, tile = collect(group, stage)
        newest = stage - 1
        norms, inverse, gram = state["norms"], state["inverse"], state["gram"]
        if stage == 0:
            gram[0, 0] = unpack(tile, 1)[0]
            norms.append(jnp.sqrt(gram[0, 0] + EPS))
            inverse.append(1.0 / norms[0])
            put(images, group, 0, pieces)
            return pieces
        found = unpack(tile, stage if stage == 1 else 2 * stage)
        if stage > 1:
            for i in range(stage):
                gram[i, newest] = gram[newest, i] = found[stage + i]
            norms.append(jnp.sqrt(gram[newest, newest] + EPS))
            inverse.append(1.0 / norms[newest])
        column = [found[i] * inverse[i] * inverse[newest] for i in range(stage)]
        state["columns"].append(column)
        coeffs = [column[i] * inverse[i] for i in range(stage)]
        pieces = combine(
            pieces, inverse[newest], coeffs, [get(images, group, i) for i in range(stage)]
        )
        put(images, group, stage, pieces)
        fresh = combine(
            get(images, group, newest),
            inverse[newest],
            coeffs,
            [get(basis, group, i) for i in range(stage)],
        )
        put(basis, group, stage, fresh)
        return pieces

    def advance(group, stage, state):
        pieces = absorb(group, stage - 1, state)
        set_lhs(group, pieces)
        vectors = [get(basis, group, i) for i in range(stage)]
        products = [(v, pieces) for v in vectors]
        if stage > 1:
            products += [(v, vectors[-1]) for v in vectors]
        stamp(group, pack(products))

    inputs[0].wait()
    states = [begin(group) for group in range(GROUPS)]
    arrived()
    apply(tuple(range(GROUPS)), 0, None)
    for group in range(GROUPS):
        flush(group, 0)
    pending = None
    for stage in range(1, ITERS):
        for group in range(GROUPS):
            advance(group, stage, states[group])
            apply((group,), stage, pending)
            pending = (group, stage)
    flush(*pending)

    for copy in inputs[1:]:
        copy.wait()
    last = ITERS - 1
    for group in range(GROUPS):
        image = absorb(group, last, states[group])
        vectors = [get(basis, group, i) for i in range(ITERS)]
        products = [(v, image) for v in vectors] + [(v, vectors[last]) for v in vectors]
        small_out[group] = pack(products + [(image, image)])
        small_start(group)

    terms = [jnp.zeros((1, LANES), F32) for _ in range(chunks)]
    for group in range(GROUPS):
        found = unpack(small_wait(group), 2 * ITERS + 1)
        norms, inverse = states[group]["norms"], states[group]["inverse"]
        gram, columns = states[group]["gram"], states[group]["columns"]
        for i in range(ITERS):
            gram[i, last] = gram[last, i] = found[ITERS + i]
        norms.append(jnp.sqrt(gram[last, last] + EPS))
        inverse.append(1.0 / norms[last])
        column = [found[i] * inverse[i] * inverse[last] for i in range(ITERS)]
        square = found[2 * ITERS] * inverse[last] * inverse[last]
        scaled = [column[i] * inverse[i] for i in range(ITERS)]
        for i in range(ITERS):
            inside = -2.0 * column[i]
            for j in range(ITERS):
                inside = inside + gram[i, j] * inverse[i] * scaled[j]
            square = square + column[i] * inside
        columns.append(column)
        lengths = norms[1:] + [jnp.sqrt(jnp.maximum(square, 0.0) + EPS)]
        columns = [columns[j] + [lengths[j]] for j in range(ITERS)]
        weights = givens_solve(columns, norms[0])
        solved = None
        for j in range(ITERS):
            scale = tall(weights[j] * inverse[j])
            part = [scale * p for p in get(basis, group, j)]
            solved = part if solved is None else [s + p for s, p in zip(solved, part)]
        for c in range(chunks):
            here = slice(c * LANES, (c + 1) * LANES)
            first = group * excite
            field[first : first + excite, here] = solved[c][:excite]
            field[total_excite + first : total_excite + first + excite, here] = solved[c][excite:]
            sens_r, sens_i = sens[0:1, here], sens[1:2, here]
            current = source_rows(currents, group, here)
            load_r = sens_r * current[:excite] - sens_i * current[excite:]
            load_i = sens_r * current[excite:] + sens_i * current[:excite]
            value = solved[c][:excite] * load_r + solved[c][excite:] * load_i
            terms[c] = terms[c] - jnp.sum(value, axis=0, keepdims=True)

    stored = pltpu.make_async_copy(field, field_hbm, field_sem)
    stored.start()
    band_out[...] = jnp.concatenate(terms + [jnp.zeros((TILE - chunks, LANES), F32)], axis=0)
    total = band_out[...]
    if bands > 1:

        for step in range(1, bands):
            band_copy(step).start()
        for step in range(1, bands):
            band_copy(step).wait()
        for step in range(1, bands):
            total = total + band_in[step]
    owners = [
        owner[c * LANES : (c + 1) * LANES].astype(F32).reshape(1, LANES) for c in range(chunks)
    ]
    small_out[GROUPS] = jnp.concatenate(
        [total[0:chunks]] + owners + [jnp.zeros((TILE - 2 * chunks, LANES), F32)], axis=0
    )
    small_start(GROUPS)
    small_wait(GROUPS)
    first_design = (band * BLK + blk) * share
    mine = (first_design + lax.broadcasted_iota(jnp.int32, (share, LANES), 0)).astype(F32)
    held = jnp.zeros((share, LANES), F32)
    for step in range(BLK):
        tile = small_out[GROUPS] if step == 0 else small_in[GROUPS, step - 1]
        for c in range(chunks):
            match = tile[chunks + c : chunks + c + 1] == mine
            held = held + jnp.where(match, tile[c : c + 1], 0.0)
    held = jnp.sum(held, axis=1, keepdims=True)
    place = lax.broadcasted_iota(jnp.int32, (share, LANES), 0)
    lane = lax.broadcasted_iota(jnp.int32, (share, LANES), 1)
    design[...] = jnp.sum(jnp.where(place == lane, held, 0.0), axis=0, keepdims=True)
    stored.wait()


def body(bands, impedance, adjoint_source, currents, sensitivity, owner):
    width = impedance.shape[2]
    order = impedance.shape[3]
    excite = adjoint_source.shape[2]
    rows = 2 * excite
    chunks = width // LANES
    data = chunks * rows // GROUPS
    block = data + TILE
    wide = 2 * width
    share = DESIGN // (bands * BLK)
    vmem = pl.BlockSpec(memory_space=pltpu.VMEM)
    hbm = pl.BlockSpec(memory_space=pl.ANY)
    dma = pltpu.SemaphoreType.DMA
    field, design = pl.pallas_call(
        functools.partial(kernel, bands, share),
        out_shape=(
            jax.ShapeDtypeStruct((rows, width), F32),
            jax.ShapeDtypeStruct((1, LANES), F32),
        ),
        in_specs=[hbm] * 5,
        out_specs=(hbm, vmem),
        scratch_shapes=[
            pltpu.VMEM((rows, width), F32),
            pltpu.VMEM((rows, width), F32),
            pltpu.VMEM((2, width), F32),
            pltpu.VMEM((width,), jnp.int32),
            pltpu.VMEM((rows, width), F32),
            pltpu.VMEM((STAGING, wide, wide), F32),
            pltpu.VMEM((CHIPS, wide, wide), BF16),
            pltpu.VMEM((CHIPS, wide, wide), BF16),
            pltpu.VMEM((2, rows, wide), BF16),
            pltpu.VMEM((GROUPS, 2, CHIPS, block, LANES), F32),
            pltpu.VMEM((GROUPS, CHIPS, block, LANES), F32),
            pltpu.VMEM((GROUPS, 2, CHIPS, block, LANES), F32),
            pltpu.VMEM((GROUPS, 2, CHIPS - 1, block, LANES), F32),
            pltpu.VMEM((GROUPS, ITERS, data, LANES), F32),
            pltpu.VMEM((GROUPS, ITERS, data, LANES), F32),
            pltpu.VMEM((GROUPS + 1, TILE, LANES), F32),
            pltpu.VMEM((GROUPS + 1, BLK - 1, TILE, LANES), F32),
            pltpu.VMEM((TILE, LANES), F32),
            pltpu.VMEM((bands, TILE, LANES), F32),
            dma((STAGING,)),
            dma((4,)),
            dma,
            dma((GROUPS, CHIPS // PER_TRIP)),
            dma((GROUPS, 2, CHIPS // PER_TRIP)),
            dma((GROUPS,)),
            dma((GROUPS, 2, 2)),
            dma((GROUPS + 1,)),
            dma((GROUPS + 1,)),
            dma((bands,)),
            dma((bands,)),
        ],
        compiler_params=pltpu.CompilerParams(
            collective_id=0, has_side_effects=True, vmem_limit_bytes=60 << 20
        ),
        name="adjoint_solve",
    )(
        impedance.reshape(wide, order),
        adjoint_source.reshape(rows, width),
        currents.reshape(rows, width),
        sensitivity.reshape(2, width),
        owner,
    )
    return field.reshape(1, 2, excite, width), design[0, :share]


def solution(mesh):
    placed = (
        P("band", None, "blk", None),
        P("band", None, None, "blk"),
        P("band", None, None, "blk"),
        P("band", None, "blk"),
        P("blk"),
    )
    return jax.shard_map(
        functools.partial(body, mesh.shape["band"]),
        mesh=mesh,
        in_specs=placed,
        out_specs=(P("band", None, None, "blk"), P(("band", "blk"))),
        check_vma=False,
    )
```

```python
import functools

import jax
import jax.numpy as jnp
from jax import lax
from jax.experimental import pallas as pl
from jax.experimental.pallas import tpu as pltpu
from jax.sharding import PartitionSpec as P

ITERS = 5
DESIGN = 4096
EPS = 1e-12
CHIPS = 8
BLK = 16
LANES = 128
STAGING = 3
GROUPS = 2
PER_TRIP = 2
TILE = 8
BLOCK_Z = (2, 1, 3, 2, 0, 1, 3, 0)
BLOCK_X = (1, 1, 1, 0, 1, 0, 0, 0)
HOP_Z = (0, 1, 3, 2, 0, 1, 3)
HOP_X = (1, 0, 0, 0, 1, 0, 0)
RELAYED = 3
ACROSS = 3
ALONG = 4
DIRECT = 5
MESH = pl.DeviceIdType.MESH
F32 = jnp.float32
BF16 = jnp.bfloat16


def givens_solve(columns, beta):
    count = len(columns)
    cosines, sines, upper = [], [], []
    rhs = [beta] + [jnp.zeros_like(beta) for _ in range(count)]
    for current in range(count):
        column = list(columns[current])
        for earlier in range(current):
            top = cosines[earlier] * column[earlier] + sines[earlier] * column[earlier + 1]
            column[earlier + 1] = (
                cosines[earlier] * column[earlier + 1] - sines[earlier] * column[earlier]
            )
            column[earlier] = top
        radius = jnp.sqrt(
            column[current] * column[current] + column[current + 1] * column[current + 1]
        )
        cosines.append(column[current] / radius)
        sines.append(column[current + 1] / radius)
        column[current] = radius
        upper.append(column[: current + 1])
        rhs[current + 1] = -sines[current] * rhs[current]
        rhs[current] = cosines[current] * rhs[current]
    weights = [None] * count
    for current in reversed(range(count)):
        total = rhs[current]
        for later in range(current + 1, count):
            total = total - upper[later][current] * weights[later]
        weights[current] = total / upper[current][current]
    return weights


def pick(values, step):
    if isinstance(step, int):
        return values[step]
    total = jnp.int32(0)
    for place, value in enumerate(values):
        if value:
            total = total + jnp.where(step == place, value, 0)
    return total


def kernel(
    bands,
    share,
    panel,
    source_hbm,
    currents_hbm,
    sens_hbm,
    owner_hbm,
    field_hbm,
    design,
    source,
    currents,
    sens,
    owner,
    field,
    staging,
    high,
    low,
    lhs,
    both,
    summed,
    pair_in,
    ring_in,
    basis,
    images,
    small_out,
    small_in,
    band_out,
    band_in,
    load_sem,
    input_sem,
    field_sem,
    pair_send,
    pair_recv,
    ring_send,
    ring_recv,
    small_send,
    small_recv,
    band_send,
    band_recv,
):
    total_excite = source.shape[0] // 2
    excite = total_excite // GROUPS
    rows = 2 * excite
    width = source.shape[1]
    chunks = width // LANES
    data = chunks * rows
    payload = data + 1
    wide = 2 * width
    trips = CHIPS // PER_TRIP
    band = lax.axis_index("band")
    blk = lax.axis_index("blk")
    core = blk % 2
    partner = blk + 1 - 2 * core
    along_x = (blk // 2) % 2
    along_z = blk // 4
    beside = band + 1 - 2 * (band % 2)

    def chip_of(step):
        return ((along_z + pick(BLOCK_Z, step)) % 4) * 2 + (along_x + pick(BLOCK_X, step)) % 2

    def next_chip(step):
        return ((along_z + pick(HOP_Z, step)) % 4) * 2 + (along_x + pick(HOP_X, step)) % 2

    def load(step):
        slot = step % STAGING
        cols = pl.ds(pl.multiple_of(chip_of(step) * wide, wide), wide)
        return pltpu.make_async_copy(panel.at[:, cols], staging.at[slot], load_sem.at[slot])

    pairs = [(source_hbm, source), (currents_hbm, currents), (sens_hbm, sens), (owner_hbm, owner)]
    inputs = [
        pltpu.make_async_copy(src, dst, input_sem.at[i]) for i, (src, dst) in enumerate(pairs)
    ]
    inputs[0].start()
    for step in range(STAGING):
        load(step).start()
    for copy in inputs[1:]:
        copy.start()

    barrier = pltpu.get_barrier_semaphore()

    def greet_blk(step, carry):
        pl.semaphore_signal(
            barrier, inc=1, device_id={"blk": (blk + step) % BLK}, device_id_type=MESH
        )
        return carry

    def greet_band(step, carry):
        pl.semaphore_signal(
            barrier, inc=1, device_id={"band": (band + step) % bands}, device_id_type=MESH
        )
        return carry

    lax.fori_loop(1, BLK, greet_blk, 0)
    if bands > 1:
        lax.fori_loop(1, bands, greet_band, 0)
        for n in range(CHIPS):
            far = ((along_z + n // 2) % 4) * 4 + ((along_x + 1) % 2) * 2 + (core + n % 2) % 2
            pl.semaphore_signal(
                barrier, inc=1, device_id={"band": beside, "blk": far}, device_id_type=MESH
            )

    def arrived():
        pl.semaphore_wait(barrier, BLK - 1 + (bands - 1 + CHIPS if bands > 1 else 0))

    def pair_copy(group, trip, parity):
        here = pl.ds(trip * PER_TRIP, PER_TRIP)
        return pltpu.make_async_remote_copy(
            src_ref=both.at[group, 1 - core, here, pl.ds(0, payload)],
            dst_ref=pair_in.at[group, parity, here, pl.ds(0, payload)],
            send_sem=pair_send.at[group, trip],
            recv_sem=pair_recv.at[group, parity, trip],
            device_id={"blk": partner},
            device_id_type=MESH,
        )

    def ring_copy(group, step, parity, relayed):
        return pltpu.make_async_remote_copy(
            src_ref=summed.at[group, step, pl.ds(0, payload)],
            dst_ref=ring_in.at[group, parity, step, pl.ds(0, payload)],
            send_sem=ring_send.at[group],
            recv_sem=ring_recv.at[group, parity, relayed],
            device_id={"blk": next_chip(step) * 2 + core},
            device_id_type=MESH,
        )

    def ring_whole(group, parity, first, count, relayed):
        whole = ring_in.at[group, parity, pl.ds(first, count), pl.ds(0, payload)]
        return pltpu.make_async_remote_copy(
            src_ref=whole,
            dst_ref=whole,
            send_sem=ring_send.at[group],
            recv_sem=ring_recv.at[group, parity, relayed],
            device_id={"blk": partner},
            device_id_type=MESH,
        )

    def small_copy(n, use):
        dz, dx, dc = (2, 1, 3, 0)[n // 4], 1 - (n // 2) % 2, 1 - n % 2
        target = ((along_z + dz) % 4) * 4 + ((along_x + dx) % 2) * 2 + (core + dc) % 2
        where = {"blk": target}
        if use == GROUPS and dx == 1 and bands > 1:
            where = {"band": beside, "blk": target}
        return pltpu.make_async_remote_copy(
            src_ref=small_out.at[use],
            dst_ref=small_in.at[use, n],
            send_sem=small_send.at[use],
            recv_sem=small_recv.at[use],
            device_id=where,
            device_id_type=MESH,
        )

    def band_copy(step):
        return pltpu.make_async_remote_copy(
            src_ref=band_out,
            dst_ref=band_in.at[step],
            send_sem=band_send.at[step],
            recv_sem=band_recv.at[step],
            device_id={"band": (band + step) % bands},
            device_id_type=MESH,
        )

    def small_start(use):
        for n in range(BLK - 1):
            small_copy(n, use).start()

    def small_wait(use):
        pltpu.make_async_remote_copy(
            src_ref=small_in.at[use],
            dst_ref=small_in.at[use],
            send_sem=small_send.at[use],
            recv_sem=small_recv.at[use],
            device_id={"blk": partner},
            device_id_type=MESH,
        ).wait()
        total = small_out[use]
        for n in range(BLK - 1):
            total = total + small_in[use, n]
        return total

    def set_lhs(group, pieces):
        swapped = [jnp.concatenate([p[excite:], -p[:excite]], axis=0) for p in pieces]
        for place, piece in enumerate(list(pieces) + swapped):
            cols = slice(place * LANES, (place + 1) * LANES)
            top = piece.astype(BF16)
            lhs[0, group * rows : (group + 1) * rows, cols] = top
            lhs[1, group * rows : (group + 1) * rows, cols] = (piece - top.astype(F32)).astype(
                BF16
            )

    def split(step):
        slot = step % STAGING
        load(step).wait()

        def convert(part, carry):
            here = pl.ds(pl.multiple_of(part * 16, 16), 16)
            value = staging[slot, here, :]
            top = value.astype(BF16)
            high[step, here, :] = top
            low[step, here, :] = (value - top.astype(F32)).astype(BF16)
            return carry

        lax.fori_loop(0, 2 * width // 16, convert, 0, unroll=4)

        @pl.when(step + STAGING < CHIPS)
        def _():
            load(step + STAGING).start()

    def multiply(groups, step):
        span = slice(groups[0] * rows, (groups[-1] + 1) * rows)
        count = len(groups) * rows
        left = jnp.concatenate([lhs[0, span, :], lhs[1, span, :]], axis=0)
        first = jnp.dot(left, high[step], preferred_element_type=F32)
        second = jnp.dot(lhs[0, span, :], low[step], preferred_element_type=F32)
        image = first[:count] + first[count:] + second
        for place, group in enumerate(groups):
            for dest in range(2):
                for chunk in range(chunks):
                    lane = (dest * chunks + chunk) * LANES
                    both[group, dest, step, chunk * rows : (chunk + 1) * rows, :] = image[
                        place * rows : (place + 1) * rows, lane : lane + LANES
                    ]

    def add_pair(group, trip, parity):
        pair_copy(group, trip, parity).wait()
        for part in range(PER_TRIP):
            step = trip * PER_TRIP + part
            summed[group, step] = both[group, core, step] + pair_in[group, parity, step]

    def forward(group, trip, parity):
        add_pair(group, trip, parity)
        for part in range(PER_TRIP):
            step = trip * PER_TRIP + part

            @pl.when(step < RELAYED)
            def _():
                ring_copy(group, step, parity, 1).start()

            @pl.when(step >= DIRECT)
            def _():
                ring_copy(group, step, parity, 0).start()

    def flush(group, stage):
        parity = stage % 2
        add_pair(group, trips - 1, parity)
        ring_copy(group, CHIPS - 2, parity, 0).start()
        ring_whole(group, parity, 0, RELAYED, 1).wait_recv()
        summed[group, ACROSS] = summed[group, ACROSS] + ring_in[group, parity, 0]
        ring_copy(group, ACROSS, parity, 0).start()
        summed[group, ALONG] = (
            summed[group, ALONG] + ring_in[group, parity, 1] + ring_in[group, parity, 2]
        )
        ring_copy(group, ALONG, parity, 0).start()

    def apply(groups, stage, pending):
        parity = stage % 2

        def each(trip, between):
            if stage == 0:
                for part in range(PER_TRIP):
                    split(trip * PER_TRIP + part)
            for part in range(PER_TRIP):
                multiply(groups, trip * PER_TRIP + part)
            for group in groups:
                pair_copy(group, trip, parity).start()
            if between is not None:
                flush(*between)

        def body(trip, carry):
            each(trip, None)
            for group in groups:
                forward(group, trip - 1, parity)
            return carry

        each(0, pending)
        lax.fori_loop(1, trips, body, 0)

    def collect(group, stage):
        parity = stage % 2
        ring_whole(group, parity, RELAYED, CHIPS - 1 - RELAYED, 0).wait_recv()
        ring_whole(group, parity, 0, CHIPS - 1, 0).wait_send()

        def gather(here):
            total = summed[group, CHIPS - 1, here, :]
            for step in range(RELAYED, CHIPS - 1):
                total = total + ring_in[group, parity, step, here, :]
            return total

        tile = gather(slice(data, data + 1))
        pieces = [gather(slice(c * rows, (c + 1) * rows)) for c in range(chunks)]
        return pieces, tile

    def get(store, group, index):
        return [store[group, index, c * rows : (c + 1) * rows, :] for c in range(chunks)]

    def put(store, group, index, pieces):
        for c in range(chunks):
            store[group, index, c * rows : (c + 1) * rows, :] = pieces[c]

    lane_of = lax.broadcasted_iota(jnp.int32, (excite, LANES), 1)
    row_of = lax.broadcasted_iota(jnp.int32, (excite, LANES), 0)
    segments = LANES // excite

    def inner_local(a, b):
        total = a[0] * b[0]
        for c in range(1, chunks):
            total = total + a[c] * b[c]
        total = total[:excite] + total[excite:]
        return jnp.sum(total, axis=1, keepdims=True)

    def pack(products):
        lines = []
        for first in range(0, len(products), segments):
            line = jnp.zeros((excite, LANES), F32)
            for q, (a, b) in enumerate(products[first : first + segments]):
                line = jnp.where(lane_of == row_of + q * excite, inner_local(a, b), line)
            lines.append(jnp.sum(line, axis=0, keepdims=True))
        lines.append(jnp.zeros((TILE - len(lines), LANES), F32))
        return jnp.concatenate(lines, axis=0)

    def unpack(tile, count):
        found = []
        for q in range(count):
            line = tile[q // segments : q // segments + 1]
            picked = jnp.where(lane_of == row_of + (q % segments) * excite, line, 0.0)
            value = jnp.sum(picked, axis=1, keepdims=True)
            found.append(jnp.broadcast_to(value, (excite, LANES)))
        return found

    def stamp(group, tile):
        for step in range(CHIPS):
            for dest in range(2):
                both[group, dest, step, data : data + TILE, :] = tile

    def tall(value):
        return jnp.concatenate([value, value], axis=0)

    def combine(lead, scale, coeffs, vectors):
        scale = tall(scale)
        out = [piece * scale for piece in lead]
        for coeff, vector in zip(coeffs, vectors):
            coeff = tall(coeff)
            out = [o - coeff * p for o, p in zip(out, vector)]
        return out

    def source_rows(ref, group, here):
        first = group * excite
        return jnp.concatenate(
            [
                ref[first : first + excite, here],
                ref[total_excite + first : total_excite + first + excite, here],
            ],
            axis=0,
        )

    def begin(group):
        start = [
            source_rows(source, group, slice(c * LANES, (c + 1) * LANES)) for c in range(chunks)
        ]
        put(basis, group, 0, start)
        set_lhs(group, start)
        stamp(group, pack([(start, start)]))
        return {"norms": [], "inverse": [], "gram": {}, "columns": []}

    def absorb(group, stage, state):
        pieces, tile = collect(group, stage)
        newest = stage - 1
        norms, inverse, gram = state["norms"], state["inverse"], state["gram"]
        if stage == 0:
            gram[0, 0] = unpack(tile, 1)[0]
            norms.append(jnp.sqrt(gram[0, 0] + EPS))
            inverse.append(1.0 / norms[0])
            put(images, group, 0, pieces)
            return pieces
        found = unpack(tile, stage if stage == 1 else 2 * stage)
        if stage > 1:
            for i in range(stage):
                gram[i, newest] = gram[newest, i] = found[stage + i]
            norms.append(jnp.sqrt(gram[newest, newest] + EPS))
            inverse.append(1.0 / norms[newest])
        column = [found[i] * inverse[i] * inverse[newest] for i in range(stage)]
        state["columns"].append(column)
        coeffs = [column[i] * inverse[i] for i in range(stage)]
        pieces = combine(
            pieces, inverse[newest], coeffs, [get(images, group, i) for i in range(stage)]
        )
        put(images, group, stage, pieces)
        fresh = combine(
            get(images, group, newest),
            inverse[newest],
            coeffs,
            [get(basis, group, i) for i in range(stage)],
        )
        put(basis, group, stage, fresh)
        return pieces

    def advance(group, stage, state):
        pieces = absorb(group, stage - 1, state)
        set_lhs(group, pieces)
        vectors = [get(basis, group, i) for i in range(stage)]
        products = [(v, pieces) for v in vectors]
        if stage > 1:
            products += [(v, vectors[-1]) for v in vectors]
        stamp(group, pack(products))

    inputs[0].wait()
    states = [begin(group) for group in range(GROUPS)]
    arrived()
    apply(tuple(range(GROUPS)), 0, None)
    for group in range(GROUPS):
        flush(group, 0)
    pending = None
    for stage in range(1, ITERS):
        for group in range(GROUPS):
            advance(group, stage, states[group])
            apply((group,), stage, pending)
            pending = (group, stage)
    flush(*pending)

    for copy in inputs[1:]:
        copy.wait()
    last = ITERS - 1
    for group in range(GROUPS):
        image = absorb(group, last, states[group])
        vectors = [get(basis, group, i) for i in range(ITERS)]
        products = [(v, image) for v in vectors] + [(v, vectors[last]) for v in vectors]
        small_out[group] = pack(products + [(image, image)])
        small_start(group)

    terms = [jnp.zeros((1, LANES), F32) for _ in range(chunks)]
    for group in range(GROUPS):
        found = unpack(small_wait(group), 2 * ITERS + 1)
        norms, inverse = states[group]["norms"], states[group]["inverse"]
        gram, columns = states[group]["gram"], states[group]["columns"]
        for i in range(ITERS):
            gram[i, last] = gram[last, i] = found[ITERS + i]
        norms.append(jnp.sqrt(gram[last, last] + EPS))
        inverse.append(1.0 / norms[last])
        column = [found[i] * inverse[i] * inverse[last] for i in range(ITERS)]
        square = found[2 * ITERS] * inverse[last] * inverse[last]
        scaled = [column[i] * inverse[i] for i in range(ITERS)]
        for i in range(ITERS):
            inside = -2.0 * column[i]
            for j in range(ITERS):
                inside = inside + gram[i, j] * inverse[i] * scaled[j]
            square = square + column[i] * inside
        columns.append(column)
        lengths = norms[1:] + [jnp.sqrt(jnp.maximum(square, 0.0) + EPS)]
        columns = [columns[j] + [lengths[j]] for j in range(ITERS)]
        weights = givens_solve(columns, norms[0])
        solved = None
        for j in range(ITERS):
            scale = tall(weights[j] * inverse[j])
            part = [scale * p for p in get(basis, group, j)]
            solved = part if solved is None else [s + p for s, p in zip(solved, part)]
        for c in range(chunks):
            here = slice(c * LANES, (c + 1) * LANES)
            first = group * excite
            field[first : first + excite, here] = solved[c][:excite]
            field[total_excite + first : total_excite + first + excite, here] = solved[c][excite:]
            sens_r, sens_i = sens[0:1, here], sens[1:2, here]
            current = source_rows(currents, group, here)
            load_r = sens_r * current[:excite] - sens_i * current[excite:]
            load_i = sens_r * current[excite:] + sens_i * current[:excite]
            value = solved[c][:excite] * load_r + solved[c][excite:] * load_i
            terms[c] = terms[c] - jnp.sum(value, axis=0, keepdims=True)

    stored = pltpu.make_async_copy(field, field_hbm, field_sem)
    stored.start()
    band_out[...] = jnp.concatenate(terms + [jnp.zeros((TILE - chunks, LANES), F32)], axis=0)
    total = band_out[...]
    if bands > 1:

        for step in range(1, bands):
            band_copy(step).start()
        for step in range(1, bands):
            band_copy(step).wait()
        for step in range(1, bands):
            total = total + band_in[step]
    owners = [
        owner[c * LANES : (c + 1) * LANES].astype(F32).reshape(1, LANES) for c in range(chunks)
    ]
    small_out[GROUPS] = jnp.concatenate(
        [total[0:chunks]] + owners + [jnp.zeros((TILE - 2 * chunks, LANES), F32)], axis=0
    )
    small_start(GROUPS)
    small_wait(GROUPS)
    first_design = (band * BLK + blk) * share
    mine = (first_design + lax.broadcasted_iota(jnp.int32, (share, LANES), 0)).astype(F32)
    held = jnp.zeros((share, LANES), F32)
    for step in range(BLK):
        tile = small_out[GROUPS] if step == 0 else small_in[GROUPS, step - 1]
        for c in range(chunks):
            match = tile[chunks + c : chunks + c + 1] == mine
            held = held + jnp.where(match, tile[c : c + 1], 0.0)
    held = jnp.sum(held, axis=1, keepdims=True)
    place = lax.broadcasted_iota(jnp.int32, (share, LANES), 0)
    lane = lax.broadcasted_iota(jnp.int32, (share, LANES), 1)
    design[...] = jnp.sum(jnp.where(place == lane, held, 0.0), axis=0, keepdims=True)
    stored.wait()


def hand_out(share, field, design, field_out, design_out):
    field_out[...] = field[...]
    design_out[...] = design[0, 0:share]


def body(bands, impedance, adjoint_source, currents, sensitivity, owner):
    width = impedance.shape[2]
    order = impedance.shape[3]
    excite = adjoint_source.shape[2]
    rows = 2 * excite
    chunks = width // LANES
    data = chunks * rows // GROUPS
    block = data + TILE
    wide = 2 * width
    share = DESIGN // (bands * BLK)
    vmem = pl.BlockSpec(memory_space=pltpu.VMEM)
    hbm = pl.BlockSpec(memory_space=pl.ANY)
    dma = pltpu.SemaphoreType.DMA
    field, design = pl.pallas_call(
        functools.partial(kernel, bands, share),
        out_shape=(
            jax.ShapeDtypeStruct((rows, width), F32),
            jax.ShapeDtypeStruct((1, LANES), F32),
        ),
        in_specs=[hbm] * 5,
        out_specs=(hbm, vmem),
        scratch_shapes=[
            pltpu.VMEM((rows, width), F32),
            pltpu.VMEM((rows, width), F32),
            pltpu.VMEM((2, width), F32),
            pltpu.VMEM((width,), jnp.int32),
            pltpu.VMEM((rows, width), F32),
            pltpu.VMEM((STAGING, wide, wide), F32),
            pltpu.VMEM((CHIPS, wide, wide), BF16),
            pltpu.VMEM((CHIPS, wide, wide), BF16),
            pltpu.VMEM((2, rows, wide), BF16),
            pltpu.VMEM((GROUPS, 2, CHIPS, block, LANES), F32),
            pltpu.VMEM((GROUPS, CHIPS, block, LANES), F32),
            pltpu.VMEM((GROUPS, 2, CHIPS, block, LANES), F32),
            pltpu.VMEM((GROUPS, 2, CHIPS - 1, block, LANES), F32),
            pltpu.VMEM((GROUPS, ITERS, data, LANES), F32),
            pltpu.VMEM((GROUPS, ITERS, data, LANES), F32),
            pltpu.VMEM((GROUPS + 1, TILE, LANES), F32),
            pltpu.VMEM((GROUPS + 1, BLK - 1, TILE, LANES), F32),
            pltpu.VMEM((TILE, LANES), F32),
            pltpu.VMEM((bands, TILE, LANES), F32),
            dma((STAGING,)),
            dma((4,)),
            dma,
            dma((GROUPS, CHIPS // PER_TRIP)),
            dma((GROUPS, 2, CHIPS // PER_TRIP)),
            dma((GROUPS,)),
            dma((GROUPS, 2, 2)),
            dma((GROUPS + 1,)),
            dma((GROUPS + 1,)),
            dma((bands,)),
            dma((bands,)),
        ],
        compiler_params=pltpu.CompilerParams(
            collective_id=0, has_side_effects=True, vmem_limit_bytes=60 << 20
        ),
        name="adjoint_solve",
    )(
        impedance.reshape(wide, order),
        adjoint_source.reshape(rows, width),
        currents.reshape(rows, width),
        sensitivity.reshape(2, width),
        owner,
    )
    field, design = pl.pallas_call(
        functools.partial(hand_out, share),
        out_shape=(
            jax.ShapeDtypeStruct((rows, width), F32),
            jax.ShapeDtypeStruct((share,), F32),
        ),
        in_specs=[vmem, vmem],
        out_specs=(vmem, vmem),
        name="hand_out",
    )(field, design)
    return field.reshape(1, 2, excite, width), design


def solution(mesh):
    placed = (
        P("band", None, "blk", None),
        P("band", None, None, "blk"),
        P("band", None, None, "blk"),
        P("band", None, "blk"),
        P("blk"),
    )
    return jax.shard_map(
        functools.partial(body, mesh.shape["band"]),
        mesh=mesh,
        in_specs=placed,
        out_specs=(P("band", None, None, "blk"), P(("band", "blk"))),
        check_vma=False,
    )
```

```python
import functools

import jax
import jax.numpy as jnp
from jax import lax
from jax.experimental import pallas as pl
from jax.experimental.pallas import tpu as pltpu
from jax.sharding import PartitionSpec as P

ITERS = 5
DESIGN = 4096
EPS = 1e-12
CHIPS = 8
BLK = 16
LANES = 128
STAGING = 3
GROUPS = 2
PER_TRIP = 2
TILE = 8
BLOCK_Z = (2, 1, 3, 2, 0, 1, 3, 0)
BLOCK_X = (1, 1, 1, 0, 1, 0, 0, 0)
HOP_Z = (0, 1, 3, 2, 0, 1, 3)
HOP_X = (1, 0, 0, 0, 1, 0, 0)
RELAYED = 3
ACROSS = 3
ALONG = 4
DIRECT = 5
MESH = pl.DeviceIdType.MESH
F32 = jnp.float32
BF16 = jnp.bfloat16


def givens_solve(columns, beta):
    count = len(columns)
    cosines, sines, upper = [], [], []
    rhs = [beta] + [jnp.zeros_like(beta) for _ in range(count)]
    for current in range(count):
        column = list(columns[current])
        for earlier in range(current):
            top = cosines[earlier] * column[earlier] + sines[earlier] * column[earlier + 1]
            column[earlier + 1] = (
                cosines[earlier] * column[earlier + 1] - sines[earlier] * column[earlier]
            )
            column[earlier] = top
        radius = jnp.sqrt(
            column[current] * column[current] + column[current + 1] * column[current + 1]
        )
        cosines.append(column[current] / radius)
        sines.append(column[current + 1] / radius)
        column[current] = radius
        upper.append(column[: current + 1])
        rhs[current + 1] = -sines[current] * rhs[current]
        rhs[current] = cosines[current] * rhs[current]
    weights = [None] * count
    for current in reversed(range(count)):
        total = rhs[current]
        for later in range(current + 1, count):
            total = total - upper[later][current] * weights[later]
        weights[current] = total / upper[current][current]
    return weights


def pick(values, step):
    if isinstance(step, int):
        return values[step]
    total = jnp.int32(0)
    for place, value in enumerate(values):
        if value:
            total = total + jnp.where(step == place, value, 0)
    return total


def kernel(
    bands,
    share,
    panel,
    source_hbm,
    currents_hbm,
    sens_hbm,
    owner_hbm,
    field_hbm,
    design,
    source,
    currents,
    sens,
    owner,
    field,
    staging,
    high,
    low,
    lhs,
    both,
    summed,
    pair_in,
    ring_in,
    basis,
    images,
    small_out,
    small_in,
    band_out,
    band_in,
    load_sem,
    input_sem,
    field_sem,
    pair_send,
    pair_recv,
    ring_send,
    ring_recv,
    small_send,
    small_recv,
    band_send,
    band_recv,
):
    total_excite = source.shape[0] // 2
    excite = total_excite // GROUPS
    rows = 2 * excite
    width = source.shape[1]
    chunks = width // LANES
    data = chunks * rows
    payload = data + 1
    wide = 2 * width
    trips = CHIPS // PER_TRIP
    band = lax.axis_index("band")
    blk = lax.axis_index("blk")
    core = blk % 2
    partner = blk + 1 - 2 * core
    along_x = (blk // 2) % 2
    along_z = blk // 4
    beside = band + 1 - 2 * (band % 2)

    def chip_of(step):
        return ((along_z + pick(BLOCK_Z, step)) % 4) * 2 + (along_x + pick(BLOCK_X, step)) % 2

    def next_chip(step):
        return ((along_z + pick(HOP_Z, step)) % 4) * 2 + (along_x + pick(HOP_X, step)) % 2

    def load(step):
        slot = step % STAGING
        cols = pl.ds(pl.multiple_of(chip_of(step) * wide, wide), wide)
        return pltpu.make_async_copy(panel.at[:, cols], staging.at[slot], load_sem.at[slot])

    pairs = [(source_hbm, source), (currents_hbm, currents), (sens_hbm, sens), (owner_hbm, owner)]
    inputs = [
        pltpu.make_async_copy(src, dst, input_sem.at[i]) for i, (src, dst) in enumerate(pairs)
    ]
    inputs[0].start()
    for step in range(STAGING):
        load(step).start()
    for copy in inputs[1:]:
        copy.start()

    barrier = pltpu.get_barrier_semaphore()

    def greet_blk(step, carry):
        pl.semaphore_signal(
            barrier, inc=1, device_id={"blk": (blk + step) % BLK}, device_id_type=MESH
        )
        return carry

    def greet_band(step, carry):
        pl.semaphore_signal(
            barrier, inc=1, device_id={"band": (band + step) % bands}, device_id_type=MESH
        )
        return carry

    lax.fori_loop(1, BLK, greet_blk, 0)
    if bands > 1:
        lax.fori_loop(1, bands, greet_band, 0)
        for n in range(CHIPS):
            far = ((along_z + n // 2) % 4) * 4 + ((along_x + 1) % 2) * 2 + (core + n % 2) % 2
            pl.semaphore_signal(
                barrier, inc=1, device_id={"band": beside, "blk": far}, device_id_type=MESH
            )

    def arrived():
        pl.semaphore_wait(barrier, BLK - 1 + (bands - 1 + CHIPS if bands > 1 else 0))

    def pair_copy(group, trip, parity):
        here = pl.ds(trip * PER_TRIP, PER_TRIP)
        return pltpu.make_async_remote_copy(
            src_ref=both.at[group, 1 - core, here, pl.ds(0, payload)],
            dst_ref=pair_in.at[group, parity, here, pl.ds(0, payload)],
            send_sem=pair_send.at[group, trip],
            recv_sem=pair_recv.at[group, parity, trip],
            device_id={"blk": partner},
            device_id_type=MESH,
        )

    def ring_copy(group, step, parity, relayed):
        return pltpu.make_async_remote_copy(
            src_ref=summed.at[group, step, pl.ds(0, payload)],
            dst_ref=ring_in.at[group, parity, step, pl.ds(0, payload)],
            send_sem=ring_send.at[group],
            recv_sem=ring_recv.at[group, parity, relayed],
            device_id={"blk": next_chip(step) * 2 + core},
            device_id_type=MESH,
        )

    def ring_whole(group, parity, first, count, relayed):
        whole = ring_in.at[group, parity, pl.ds(first, count), pl.ds(0, payload)]
        return pltpu.make_async_remote_copy(
            src_ref=whole,
            dst_ref=whole,
            send_sem=ring_send.at[group],
            recv_sem=ring_recv.at[group, parity, relayed],
            device_id={"blk": partner},
            device_id_type=MESH,
        )

    def lines_of(use):
        if use == GROUPS:
            return 2 * chunks
        return pl.cdiv(2 * ITERS + 1, LANES // excite)

    def small_copy(n, use):
        dz, dx, dc = (2, 1, 3, 0)[n // 4], 1 - (n // 2) % 2, 1 - n % 2
        target = ((along_z + dz) % 4) * 4 + ((along_x + dx) % 2) * 2 + (core + dc) % 2
        where = {"blk": target}
        if use == GROUPS and dx == 1 and bands > 1:
            where = {"band": beside, "blk": target}
        return pltpu.make_async_remote_copy(
            src_ref=small_out.at[use, pl.ds(0, lines_of(use))],
            dst_ref=small_in.at[use, n, pl.ds(0, lines_of(use))],
            send_sem=small_send.at[use],
            recv_sem=small_recv.at[use],
            device_id=where,
            device_id_type=MESH,
        )

    def band_copy(step):
        return pltpu.make_async_remote_copy(
            src_ref=band_out.at[pl.ds(0, chunks)],
            dst_ref=band_in.at[step, pl.ds(0, chunks)],
            send_sem=band_send.at[step],
            recv_sem=band_recv.at[step],
            device_id={"band": (band + step) % bands},
            device_id_type=MESH,
        )

    def small_start(use):
        for n in range(BLK - 1):
            small_copy(n, use).start()

    def small_wait(use):
        pltpu.make_async_remote_copy(
            src_ref=small_in.at[use, :, pl.ds(0, lines_of(use))],
            dst_ref=small_in.at[use, :, pl.ds(0, lines_of(use))],
            send_sem=small_send.at[use],
            recv_sem=small_recv.at[use],
            device_id={"blk": partner},
            device_id_type=MESH,
        ).wait()
        total = small_out[use]
        for n in range(BLK - 1):
            total = total + small_in[use, n]
        return total

    def set_lhs(group, pieces):
        swapped = [jnp.concatenate([p[excite:], -p[:excite]], axis=0) for p in pieces]
        for place, piece in enumerate(list(pieces) + swapped):
            cols = slice(place * LANES, (place + 1) * LANES)
            top = piece.astype(BF16)
            lhs[0, group * rows : (group + 1) * rows, cols] = top
            lhs[1, group * rows : (group + 1) * rows, cols] = (piece - top.astype(F32)).astype(
                BF16
            )

    def split(step):
        slot = step % STAGING
        load(step).wait()

        def convert(part, carry):
            here = pl.ds(pl.multiple_of(part * 16, 16), 16)
            value = staging[slot, here, :]
            top = value.astype(BF16)
            high[step, here, :] = top
            low[step, here, :] = (value - top.astype(F32)).astype(BF16)
            return carry

        lax.fori_loop(0, 2 * width // 16, convert, 0, unroll=4)

        @pl.when(step + STAGING < CHIPS)
        def _():
            load(step + STAGING).start()

    def multiply(groups, step):
        span = slice(groups[0] * rows, (groups[-1] + 1) * rows)
        count = len(groups) * rows
        left = jnp.concatenate([lhs[0, span, :], lhs[1, span, :]], axis=0)
        first = jnp.dot(left, high[step], preferred_element_type=F32)
        second = jnp.dot(lhs[0, span, :], low[step], preferred_element_type=F32)
        image = first[:count] + first[count:] + second
        for place, group in enumerate(groups):
            for dest in range(2):
                for chunk in range(chunks):
                    lane = (dest * chunks + chunk) * LANES
                    both[group, dest, step, chunk * rows : (chunk + 1) * rows, :] = image[
                        place * rows : (place + 1) * rows, lane : lane + LANES
                    ]

    def add_pair(group, trip, parity):
        pair_copy(group, trip, parity).wait()
        for part in range(PER_TRIP):
            step = trip * PER_TRIP + part
            summed[group, step] = both[group, core, step] + pair_in[group, parity, step]

    def forward(group, trip, parity):
        add_pair(group, trip, parity)
        for part in range(PER_TRIP):
            step = trip * PER_TRIP + part

            @pl.when(step < RELAYED)
            def _():
                ring_copy(group, step, parity, 1).start()

            @pl.when(step >= DIRECT)
            def _():
                ring_copy(group, step, parity, 0).start()

    def flush(group, stage):
        parity = stage % 2
        add_pair(group, trips - 1, parity)
        ring_copy(group, CHIPS - 2, parity, 0).start()
        ring_whole(group, parity, 0, RELAYED, 1).wait_recv()
        summed[group, ACROSS] = summed[group, ACROSS] + ring_in[group, parity, 0]
        ring_copy(group, ACROSS, parity, 0).start()
        summed[group, ALONG] = (
            summed[group, ALONG] + ring_in[group, parity, 1] + ring_in[group, parity, 2]
        )
        ring_copy(group, ALONG, parity, 0).start()

    def apply(groups, stage, pending):
        parity = stage % 2

        def each(trip, between):
            if stage == 0:
                for part in range(PER_TRIP):
                    split(trip * PER_TRIP + part)
            for part in range(PER_TRIP):
                multiply(groups, trip * PER_TRIP + part)
            for group in groups:
                pair_copy(group, trip, parity).start()
            if between is not None:
                flush(*between)

        def body(trip, carry):
            each(trip, None)
            for group in groups:
                forward(group, trip - 1, parity)
            return carry

        each(0, pending)
        lax.fori_loop(1, trips, body, 0)

    def collect(group, stage):
        parity = stage % 2
        ring_whole(group, parity, RELAYED, CHIPS - 1 - RELAYED, 0).wait_recv()
        ring_whole(group, parity, 0, CHIPS - 1, 0).wait_send()

        def gather(here):
            total = summed[group, CHIPS - 1, here, :]
            for step in range(RELAYED, CHIPS - 1):
                total = total + ring_in[group, parity, step, here, :]
            return total

        tile = gather(slice(data, data + 1))
        pieces = [gather(slice(c * rows, (c + 1) * rows)) for c in range(chunks)]
        return pieces, tile

    def get(store, group, index):
        return [store[group, index, c * rows : (c + 1) * rows, :] for c in range(chunks)]

    def put(store, group, index, pieces):
        for c in range(chunks):
            store[group, index, c * rows : (c + 1) * rows, :] = pieces[c]

    lane_of = lax.broadcasted_iota(jnp.int32, (excite, LANES), 1)
    row_of = lax.broadcasted_iota(jnp.int32, (excite, LANES), 0)
    segments = LANES // excite

    def inner_local(a, b):
        total = a[0] * b[0]
        for c in range(1, chunks):
            total = total + a[c] * b[c]
        total = total[:excite] + total[excite:]
        return jnp.sum(total, axis=1, keepdims=True)

    def pack(products):
        lines = []
        for first in range(0, len(products), segments):
            line = jnp.zeros((excite, LANES), F32)
            for q, (a, b) in enumerate(products[first : first + segments]):
                line = jnp.where(lane_of == row_of + q * excite, inner_local(a, b), line)
            lines.append(jnp.sum(line, axis=0, keepdims=True))
        lines.append(jnp.zeros((TILE - len(lines), LANES), F32))
        return jnp.concatenate(lines, axis=0)

    def unpack(tile, count):
        found = []
        for q in range(count):
            line = tile[q // segments : q // segments + 1]
            picked = jnp.where(lane_of == row_of + (q % segments) * excite, line, 0.0)
            value = jnp.sum(picked, axis=1, keepdims=True)
            found.append(jnp.broadcast_to(value, (excite, LANES)))
        return found

    def stamp(group, tile):
        for step in range(CHIPS):
            for dest in range(2):
                both[group, dest, step, data : data + TILE, :] = tile

    def tall(value):
        return jnp.concatenate([value, value], axis=0)

    def combine(lead, scale, coeffs, vectors):
        scale = tall(scale)
        out = [piece * scale for piece in lead]
        for coeff, vector in zip(coeffs, vectors):
            coeff = tall(coeff)
            out = [o - coeff * p for o, p in zip(out, vector)]
        return out

    def source_rows(ref, group, here):
        first = group * excite
        return jnp.concatenate(
            [
                ref[first : first + excite, here],
                ref[total_excite + first : total_excite + first + excite, here],
            ],
            axis=0,
        )

    def begin(group):
        start = [
            source_rows(source, group, slice(c * LANES, (c + 1) * LANES)) for c in range(chunks)
        ]
        put(basis, group, 0, start)
        set_lhs(group, start)
        stamp(group, pack([(start, start)]))
        return {"norms": [], "inverse": [], "gram": {}, "columns": []}

    def absorb(group, stage, state):
        pieces, tile = collect(group, stage)
        newest = stage - 1
        norms, inverse, gram = state["norms"], state["inverse"], state["gram"]
        if stage == 0:
            gram[0, 0] = unpack(tile, 1)[0]
            norms.append(jnp.sqrt(gram[0, 0] + EPS))
            inverse.append(1.0 / norms[0])
            put(images, group, 0, pieces)
            return pieces
        found = unpack(tile, stage if stage == 1 else 2 * stage)
        if stage > 1:
            for i in range(stage):
                gram[i, newest] = gram[newest, i] = found[stage + i]
            norms.append(jnp.sqrt(gram[newest, newest] + EPS))
            inverse.append(1.0 / norms[newest])
        column = [found[i] * inverse[i] * inverse[newest] for i in range(stage)]
        state["columns"].append(column)
        coeffs = [column[i] * inverse[i] for i in range(stage)]
        pieces = combine(
            pieces, inverse[newest], coeffs, [get(images, group, i) for i in range(stage)]
        )
        put(images, group, stage, pieces)
        fresh = combine(
            get(images, group, newest),
            inverse[newest],
            coeffs,
            [get(basis, group, i) for i in range(stage)],
        )
        put(basis, group, stage, fresh)
        return pieces

    def advance(group, stage, state):
        pieces = absorb(group, stage - 1, state)
        set_lhs(group, pieces)
        vectors = [get(basis, group, i) for i in range(stage)]
        products = [(v, pieces) for v in vectors]
        if stage > 1:
            products += [(v, vectors[-1]) for v in vectors]
        stamp(group, pack(products))

    inputs[0].wait()
    states = [begin(group) for group in range(GROUPS)]
    arrived()
    apply(tuple(range(GROUPS)), 0, None)
    flush(0, 0)
    pending = (1, 0)
    for stage in range(1, ITERS):
        for group in range(GROUPS):
            advance(group, stage, states[group])
            apply((group,), stage, pending)
            pending = (group, stage)
    flush(*pending)

    for copy in inputs[1:]:
        copy.wait()
    last = ITERS - 1
    for group in range(GROUPS):
        image = absorb(group, last, states[group])
        vectors = [get(basis, group, i) for i in range(ITERS)]
        products = [(v, image) for v in vectors] + [(v, vectors[last]) for v in vectors]
        small_out[group] = pack(products + [(image, image)])
        small_start(group)

    terms = [jnp.zeros((1, LANES), F32) for _ in range(chunks)]
    for group in range(GROUPS):
        found = unpack(small_wait(group), 2 * ITERS + 1)
        norms, inverse = states[group]["norms"], states[group]["inverse"]
        gram, columns = states[group]["gram"], states[group]["columns"]
        for i in range(ITERS):
            gram[i, last] = gram[last, i] = found[ITERS + i]
        norms.append(jnp.sqrt(gram[last, last] + EPS))
        inverse.append(1.0 / norms[last])
        column = [found[i] * inverse[i] * inverse[last] for i in range(ITERS)]
        square = found[2 * ITERS] * inverse[last] * inverse[last]
        scaled = [column[i] * inverse[i] for i in range(ITERS)]
        for i in range(ITERS):
            inside = -2.0 * column[i]
            for j in range(ITERS):
                inside = inside + gram[i, j] * inverse[i] * scaled[j]
            square = square + column[i] * inside
        columns.append(column)
        lengths = norms[1:] + [jnp.sqrt(jnp.maximum(square, 0.0) + EPS)]
        columns = [columns[j] + [lengths[j]] for j in range(ITERS)]
        weights = givens_solve(columns, norms[0])
        solved = None
        for j in range(ITERS):
            scale = tall(weights[j] * inverse[j])
            part = [scale * p for p in get(basis, group, j)]
            solved = part if solved is None else [s + p for s, p in zip(solved, part)]
        for c in range(chunks):
            here = slice(c * LANES, (c + 1) * LANES)
            first = group * excite
            field[first : first + excite, here] = solved[c][:excite]
            field[total_excite + first : total_excite + first + excite, here] = solved[c][excite:]
            sens_r, sens_i = sens[0:1, here], sens[1:2, here]
            current = source_rows(currents, group, here)
            load_r = sens_r * current[:excite] - sens_i * current[excite:]
            load_i = sens_r * current[excite:] + sens_i * current[:excite]
            value = solved[c][:excite] * load_r + solved[c][excite:] * load_i
            terms[c] = terms[c] - jnp.sum(value, axis=0, keepdims=True)

    stored = pltpu.make_async_copy(field, field_hbm, field_sem)
    stored.start()
    band_out[...] = jnp.concatenate(terms + [jnp.zeros((TILE - chunks, LANES), F32)], axis=0)
    total = band_out[...]
    if bands > 1:

        for step in range(1, bands):
            band_copy(step).start()
        for step in range(1, bands):
            band_copy(step).wait()
        for step in range(1, bands):
            total = total + band_in[step]
    owners = [
        owner[c * LANES : (c + 1) * LANES].astype(F32).reshape(1, LANES) for c in range(chunks)
    ]
    small_out[GROUPS] = jnp.concatenate(
        [total[0:chunks]] + owners + [jnp.zeros((TILE - 2 * chunks, LANES), F32)], axis=0
    )
    small_start(GROUPS)
    small_wait(GROUPS)
    first_design = (band * BLK + blk) * share
    mine = (first_design + lax.broadcasted_iota(jnp.int32, (share, LANES), 0)).astype(F32)
    held = jnp.zeros((share, LANES), F32)
    for step in range(BLK):
        tile = small_out[GROUPS] if step == 0 else small_in[GROUPS, step - 1]
        for c in range(chunks):
            match = tile[chunks + c : chunks + c + 1] == mine
            held = held + jnp.where(match, tile[c : c + 1], 0.0)
    held = jnp.sum(held, axis=1, keepdims=True)
    place = lax.broadcasted_iota(jnp.int32, (share, LANES), 0)
    lane = lax.broadcasted_iota(jnp.int32, (share, LANES), 1)
    design[...] = jnp.sum(jnp.where(place == lane, held, 0.0), axis=0, keepdims=True)
    stored.wait()


def hand_out(share, field, design, field_out, design_out):
    field_out[...] = field[...]
    design_out[...] = design[0, 0:share]


def body(bands, impedance, adjoint_source, currents, sensitivity, owner):
    width = impedance.shape[2]
    order = impedance.shape[3]
    excite = adjoint_source.shape[2]
    rows = 2 * excite
    chunks = width // LANES
    data = chunks * rows // GROUPS
    block = data + TILE
    wide = 2 * width
    share = DESIGN // (bands * BLK)
    vmem = pl.BlockSpec(memory_space=pltpu.VMEM)
    hbm = pl.BlockSpec(memory_space=pl.ANY)
    dma = pltpu.SemaphoreType.DMA
    field, design = pl.pallas_call(
        functools.partial(kernel, bands, share),
        out_shape=(
            jax.ShapeDtypeStruct((rows, width), F32),
            jax.ShapeDtypeStruct((1, LANES), F32),
        ),
        in_specs=[hbm] * 5,
        out_specs=(hbm, vmem),
        scratch_shapes=[
            pltpu.VMEM((rows, width), F32),
            pltpu.VMEM((rows, width), F32),
            pltpu.VMEM((2, width), F32),
            pltpu.VMEM((width,), jnp.int32),
            pltpu.VMEM((rows, width), F32),
            pltpu.VMEM((STAGING, wide, wide), F32),
            pltpu.VMEM((CHIPS, wide, wide), BF16),
            pltpu.VMEM((CHIPS, wide, wide), BF16),
            pltpu.VMEM((2, rows, wide), BF16),
            pltpu.VMEM((GROUPS, 2, CHIPS, block, LANES), F32),
            pltpu.VMEM((GROUPS, CHIPS, block, LANES), F32),
            pltpu.VMEM((GROUPS, 2, CHIPS, block, LANES), F32),
            pltpu.VMEM((GROUPS, 2, CHIPS - 1, block, LANES), F32),
            pltpu.VMEM((GROUPS, ITERS, data, LANES), F32),
            pltpu.VMEM((GROUPS, ITERS, data, LANES), F32),
            pltpu.VMEM((GROUPS + 1, TILE, LANES), F32),
            pltpu.VMEM((GROUPS + 1, BLK - 1, TILE, LANES), F32),
            pltpu.VMEM((TILE, LANES), F32),
            pltpu.VMEM((bands, TILE, LANES), F32),
            dma((STAGING,)),
            dma((4,)),
            dma,
            dma((GROUPS, CHIPS // PER_TRIP)),
            dma((GROUPS, 2, CHIPS // PER_TRIP)),
            dma((GROUPS,)),
            dma((GROUPS, 2, 2)),
            dma((GROUPS + 1,)),
            dma((GROUPS + 1,)),
            dma((bands,)),
            dma((bands,)),
        ],
        compiler_params=pltpu.CompilerParams(
            collective_id=0, has_side_effects=True, vmem_limit_bytes=60 << 20
        ),
        name="adjoint_solve",
    )(
        impedance.reshape(wide, order),
        adjoint_source.reshape(rows, width),
        currents.reshape(rows, width),
        sensitivity.reshape(2, width),
        owner,
    )
    field, design = pl.pallas_call(
        functools.partial(hand_out, share),
        out_shape=(
            jax.ShapeDtypeStruct((rows, width), F32),
            jax.ShapeDtypeStruct((share,), F32),
        ),
        in_specs=[vmem, vmem],
        out_specs=(vmem, vmem),
        name="hand_out",
    )(field, design)
    return field.reshape(1, 2, excite, width), design


def solution(mesh):
    placed = (
        P("band", None, "blk", None),
        P("band", None, None, "blk"),
        P("band", None, None, "blk"),
        P("band", None, "blk"),
        P("blk"),
    )
    return jax.shard_map(
        functools.partial(body, mesh.shape["band"]),
        mesh=mesh,
        in_specs=placed,
        out_specs=(P("band", None, None, "blk"), P(("band", "blk"))),
        check_vma=False,
    )
```
